32 devices in a mesh: shard: 4 (over y, x), rep: 8 (over z, core).
Axes of the slice: x: 2, y: 2, z: 4, core: 2. Of those that a mesh axis runs over, the one named last changes fastest.
Arguments:
- tokens: bfloat16 [16384, 8192], P('rep', 'shard'), may hold values from -21 to 21
- key_cotangent: bfloat16 [16384, 1024], P('rep'), may hold values from -21 to 21
- value_cotangent: bfloat16 [16384, 1024], P('rep'), may hold values from -21 to 21
- key_weight: float32 [8192, 1024], P(('shard', 'rep')), may hold values from -0.75 to 0.75
- value_weight: float32 [8192, 1024], P(('shard', 'rep')), may hold values from -0.75 to 0.75
- key_moment: float32 [8192, 1024], P(('shard', 'rep')), may hold values from -6 to 6
- value_moment: float32 [8192, 1024], P(('shard', 'rep')), may hold values from -6 to 6
Outputs:
- new_key_weight: float32 [8192, 1024], P(('shard', 'rep'))
- new_value_weight: float32 [8192, 1024], P(('shard', 'rep'))
- new_key_moment: float32 [8192, 1024], P(('shard', 'rep'))
- new_value_moment: float32 [8192, 1024], P(('shard', 'rep'))
The draws below stay inside these ranges and needn't reach their ends.
All inputs are finite; a program needn't handle non-finite values.
Results may differ from the reference program's by a relative error of at most 0.0003.
Values may be sent and summed in bfloat16 or wider, within the bound.
A program may use at most 128 MiB of HBM per device.

```python
import math
import jax
import jax.numpy as jnp
from jax import lax

D = 8192
KV = 1024
TOK_DEV = 2048
TOKENS = 16384
N_REP = 8


def shifted_draw(key, columns, column_scale):
    shift_key, noise_key = jax.random.split(key, 2)
    shift_size = 1.22 * TOK_DEV ** (-0.25)
    shifted = jnp.clip(jax.random.normal(shift_key, (columns,), jnp.float32), -4.0, 4.0) * shift_size
    jitter = jnp.clip(jax.random.normal(noise_key, (TOKENS, columns), jnp.float32), -4.0, 4.0)
    return (column_scale[None, :] * (shifted[None, :] + jitter)).astype(jnp.bfloat16)


def draw_tokens(key, part):
    folded = jax.random.fold_in(key, 11)
    position_ramp = jnp.arange(D, dtype=jnp.float32) / (D - 1)
    column_scale = 3.0 ** position_ramp
    return shifted_draw(folded, D, column_scale)


def cotangent_draw(key, salt_value):
    folded = jax.random.fold_in(key, salt_value)
    scale_key, remaining = jax.random.split(folded, 2)
    column_scale = jnp.exp(jax.random.uniform(scale_key, (KV,), jnp.float32, math.log(0.3), math.log(3.0)))
    return shifted_draw(remaining, KV, column_scale)


def draw_key_cotangent(key, part):
    return cotangent_draw(key, 23)


def draw_value_cotangent(key, part):
    return cotangent_draw(key, 37)


def block_levels(rng, dims, cuts, least, top_value):
    def one(position, blocks):
        draws = jax.random.uniform(jax.random.fold_in(jax.random.fold_in(rng, 6), position), (blocks,), jnp.float32, least / len(cuts), top_value / len(cuts))
        return jnp.repeat(jnp.exp(draws), dims[position] // blocks).reshape((-1,) + (1,) * (len(dims) - position - 1))

    factor_of = one(*cuts[0])
    for cut in cuts[1:]:
        factor_of = factor_of * one(*cut)
    return factor_of


def normal_values(rng, shape, deviation, reach, cuts=(), kind=jnp.bfloat16):
    result = deviation * jax.random.normal(rng, shape, jnp.float32)
    if cuts:
        result = result * block_levels(rng, shape, cuts, -0.22, 0.18)
    return jnp.clip(result, -reach, reach).astype(kind)


def setup_inputs(seed: int = 0) -> dict:
    seeds = jax.random.split(jax.random.key(seed), 8)
    return {
        "tokens": draw_tokens(jax.random.fold_in(seeds[7], 71), 0),
        "key_cotangent": draw_key_cotangent(jax.random.fold_in(seeds[7], 71), 0),
        "value_cotangent": draw_value_cotangent(jax.random.fold_in(seeds[7], 71), 0),
        "key_weight": normal_values(seeds[3], (D, KV), 0.05, 0.75, ((0, 32),), jnp.float32),
        "value_weight": normal_values(seeds[4], (D, KV), 0.05, 0.75, ((0, 32),), jnp.float32),
        "key_moment": normal_values(seeds[5], (D, KV), 1.0, 6.0, ((0, 32),), jnp.float32),
        "value_moment": normal_values(seeds[6], (D, KV), 1.0, 6.0, ((0, 32),), jnp.float32),
    }


EPSILON = 1e-06
MOMENTUM_DECAY = 0.9
STEP_SIZE = 0.01

def replica_grad(tokens, cotangent, replica):
    token_rows = tokens[replica * TOK_DEV:(replica + 1) * TOK_DEV]
    cotangent_rows = cotangent[replica * TOK_DEV:(replica + 1) * TOK_DEV]
    product = lax.dot_general(token_rows, cotangent_rows, (((0,), (0,)), ((), ())), preferred_element_type=jnp.float32)
    return product * (1.0 / math.sqrt(TOK_DEV))

def combine(left_part, right_part):
    cross = jnp.sum(left_part * right_part)
    left_square = jnp.sum(left_part * left_part)
    right_square = jnp.sum(right_part * right_part)
    left_coef = 1.0 - cross / (2.0 * (left_square + EPSILON))
    right_coef = 1.0 - cross / (2.0 * (right_square + EPSILON))
    return left_coef * left_part + right_coef * right_part

def merged_tree(tokens, cotangent, start_index, members):
    if members == 1:
        return replica_grad(tokens, cotangent, start_index)
    half_members = members // 2
    left_part = merged_tree(tokens, cotangent, start_index, half_members)
    right_part = merged_tree(tokens, cotangent, start_index + half_members, half_members)
    return combine(left_part, right_part)

def reference(tokens, key_cotangent, value_cotangent, key_weight, value_weight, key_moment, value_moment):
    key_merged = merged_tree(tokens, key_cotangent, 0, N_REP)
    value_merged = merged_tree(tokens, value_cotangent, 0, N_REP)
    new_key_moment = MOMENTUM_DECAY * key_moment + key_merged
    new_value_moment = MOMENTUM_DECAY * value_moment + value_merged
    new_key_weight = key_weight - STEP_SIZE * new_key_moment
    new_value_weight = value_weight - STEP_SIZE * new_value_moment
    return (new_key_weight, new_value_weight, new_key_moment, new_value_moment)
```

```python
import math

import jax
import jax.numpy as jnp
from jax import lax
from jax.sharding import PartitionSpec as P

EPSILON = 1e-06
MOMENTUM_DECAY = 0.9
STEP_SIZE = 0.01
TINY_BOUND = 1e-16
HALF_TOP = 32768.0
HALF = jnp.float16


def inner(left, right):
    return jnp.sum(left * right)


def pair_coefs(cross, first_square, second_square):
    first = 1.0 - cross / (2.0 * (first_square + EPSILON))
    second = 1.0 - cross / (2.0 * (second_square + EPSILON))
    return first, second


def slot_sum(parts, slot, slots):
    values = jnp.stack(parts)
    here = jnp.arange(slots)[:, None] == slot
    total = lax.psum(jnp.where(here, values[None, :], 0.0), ("shard", "rep"))
    return lax.dynamic_index_in_dim(total, slot, 0, keepdims=False)


def tree_coefs(gram):
    count = len(gram)
    coefs = [1.0] * count
    span = 1
    while len(gram) > 1:
        pairs = [
            pair_coefs(gram[i][i + 1], gram[i][i], gram[i + 1][i + 1])
            for i in range(0, len(gram), 2)
        ]
        for member in range(count):
            coefs[member] = coefs[member] * pairs[member // (2 * span)][member // span % 2]
        half = len(gram) // 2
        merged = [[None] * half for _ in range(half)]
        for i in range(half):
            for j in range(half):
                merged[i][j] = sum(
                    pairs[i][a] * pairs[j][b] * gram[2 * i + a][2 * j + b]
                    for a in range(2)
                    for b in range(2)
                )
        gram = merged
        span *= 2
    return coefs


def norm_bound(coefs, squares):
    bound = jnp.abs(coefs[0]) * jnp.sqrt(squares[0]) + jnp.abs(coefs[1]) * jnp.sqrt(squares[1])
    return jnp.maximum(bound, TINY_BOUND)


def move(block, route):
    return lax.ppermute(block, "rep", route)


def exchange(units, unit, count, route_of):
    blocks = [lax.dynamic_index_in_dim(units, unit, 0, keepdims=False)]
    for step in range(1, count):
        target = lax.rem(unit + step, count)
        outgoing = lax.dynamic_index_in_dim(units, target, 0, keepdims=False).astype(HALF)
        outgoing = lax.optimization_barrier(outgoing)
        blocks.append(move(outgoing, route_of(step)).astype(jnp.float32))
    return blocks


def gram_parts(blocks, unit, count, scale, owner):
    parts = []
    for i in range(count):
        for j in range(i, count):
            parts.append(((i, j), inner(blocks[i], blocks[j])))
    absolute = jnp.zeros((count, count), jnp.float32)
    order = jnp.arange(count)
    for (i, j), value in parts:
        row = order[:, None] == lax.rem(unit - i + count, count)
        column = order[None, :] == lax.rem(unit - j + count, count)
        absolute = absolute + jnp.where(row & column, value, 0.0)
        if i != j:
            absolute = absolute + jnp.where(row.T & column.T, value, 0.0)
    scales = jnp.where(order == unit, jnp.where(owner, scale, 0.0), 0.0)
    return jnp.concatenate([absolute.reshape(-1), scales])


def blend(blocks, totals, unit, count):
    scales = [totals[count * count + i] for i in range(count)]
    gram = [
        [totals[i * count + j] * (scales[i] * scales[j]) for j in range(count)]
        for i in range(count)
    ]
    coefs = tree_coefs(gram)
    weights = jnp.stack([coefs[i] * scales[i] for i in range(count)])
    merged = 0.0
    for step in range(count):
        source = lax.rem(unit - step + count, count)
        merged = merged + weights[source] * blocks[step]
    return merged


def shards(
    tokens, key_cotangent, value_cotangent, key_weight, value_weight, key_moment, value_moment
):
    replicas = lax.axis_size("rep")
    device_index = lax.axis_index("rep")
    shard_index = lax.axis_index("shard")
    groups = replicas // 2
    duos = groups // 2
    core = device_index % 2
    group = device_index // 2
    half_bit = group % 2
    duo = group // 2
    width, features = tokens.shape[1], key_cotangent.shape[1]
    block = width // replicas
    factor = 1.0 / math.sqrt(tokens.shape[0])
    cores = [(i, i ^ 1) for i in range(replicas)]

    def grad(cotangent):
        product = lax.dot_general(
            tokens, cotangent, (((0,), (0,)), ((), ())), preferred_element_type=jnp.float32
        )
        return (product * factor).reshape(groups, 2, block, features)

    def swap_cores(full):
        kept = lax.dynamic_index_in_dim(full, core, 1, keepdims=False)
        outgoing = lax.dynamic_index_in_dim(full, 1 - core, 1, keepdims=False)
        return kept, move(outgoing, cores)

    value_full = grad(value_cotangent)
    value_kept, value_arrived = swap_cores(value_full)
    key_full = grad(key_cotangent)
    key_kept, key_arrived = swap_cores(key_full)
    is_first = core == 0

    def duel_parts(kept, arrived):
        own, other = inner(kept, kept), inner(arrived, arrived)
        return [
            inner(kept, arrived),
            jnp.where(is_first, own, other),
            jnp.where(is_first, other, own),
        ]

    totals = slot_sum(
        duel_parts(value_kept, value_arrived) + duel_parts(key_kept, key_arrived), group, groups
    )

    def scaled_duel(kept, arrived, sums):
        first, second = pair_coefs(sums[0], sums[1], sums[2])
        scale = norm_bound((first, second), (sums[1], sums[2])) / HALF_TOP
        own = jnp.where(is_first, first, second) / scale
        other = jnp.where(is_first, second, first) / scale
        return own * kept + other * arrived, scale

    value_units, value_scale = scaled_duel(value_kept, value_arrived, totals[:3])
    key_units, key_scale = scaled_duel(key_kept, key_arrived, totals[3:])
    owner = (shard_index == 0) & (core == 0)

    value_units = value_units.reshape(duos, 2, block, features)
    kept = lax.dynamic_index_in_dim(value_units, half_bit, 1, keepdims=False)
    outgoing = lax.dynamic_index_in_dim(value_units, 1 - half_bit, 1, keepdims=False).astype(HALF)
    outgoing = lax.optimization_barrier(outgoing)
    arrived = move(outgoing, [(i, i ^ 2) for i in range(replicas)]).astype(jnp.float32)

    def group_route(step):
        return [
            (2 * g + c, 2 * ((g + step) % groups) + c) for g in range(groups) for c in range(2)
        ]

    def duo_route(step):
        return [
            (4 * d + c, 4 * ((d + step) % duos) + c) for d in range(duos) for c in range(4)
        ]

    key_blocks = exchange(key_units, group, groups, group_route)

    even = half_bit == 0
    own, other = inner(kept, kept), inner(arrived, arrived)
    sums = slot_sum(
        [
            inner(kept, arrived),
            jnp.where(even, own, other),
            jnp.where(even, other, own),
            jnp.where(owner & even, value_scale, 0.0),
            jnp.where(owner & ~even, value_scale, 0.0),
        ],
        duo,
        duos,
    )
    squares = (sums[1] * (sums[3] * sums[3]), sums[2] * (sums[4] * sums[4]))
    first, second = pair_coefs(sums[0] * (sums[3] * sums[4]), squares[0], squares[1])
    duo_scale = norm_bound((first, second), squares) / HALF_TOP
    first, second = first * sums[3] / duo_scale, second * sums[4] / duo_scale
    duo_units = jnp.where(even, first, second) * kept + jnp.where(even, second, first) * arrived
    value_blocks = exchange(duo_units, duo, duos, duo_route)

    key_sums = gram_parts(key_blocks, group, groups, key_scale, owner)
    value_sums = gram_parts(value_blocks, duo, duos, duo_scale, owner & even)
    sums = lax.psum(jnp.concatenate([key_sums, value_sums]), ("shard", "rep"))
    key_merged = blend(key_blocks, sums[: key_sums.shape[0]], group, groups)
    value_merged = blend(value_blocks, sums[key_sums.shape[0] :], duo, duos)

    new_key_moment = MOMENTUM_DECAY * key_moment + key_merged
    new_value_moment = MOMENTUM_DECAY * value_moment + value_merged
    new_key_weight = key_weight - STEP_SIZE * new_key_moment
    new_value_weight = value_weight - STEP_SIZE * new_value_moment
    return (new_key_weight, new_value_weight, new_key_moment, new_value_moment)


def solution(mesh):
    grads = (P("rep", None),) * 2
    rows = (P(("shard", "rep"), None),) * 4
    return jax.shard_map(
        shards, mesh=mesh, in_specs=(P("rep", "shard"),) + grads + rows, out_specs=rows,
        check_vma=False,
    )
```

```python
import functools
import math

import jax
import jax.numpy as jnp
from jax import lax
from jax.experimental import pallas as pl
from jax.experimental.pallas import tpu as pltpu
from jax.sharding import PartitionSpec as P

EPSILON = 1e-06
MOMENTUM_DECAY = 0.9
STEP_SIZE = 0.01
TINY_BOUND = 1e-16
HALF_TOP = 32768.0
HALF = jnp.float16
TILE = (8, 128)


def pair_coefs(cross, first_square, second_square):
    first = 1.0 - cross / (2.0 * (first_square + EPSILON))
    second = 1.0 - cross / (2.0 * (second_square + EPSILON))
    return first, second


def tree_coefs(gram):
    count = len(gram)
    coefs = [1.0] * count
    span = 1
    while len(gram) > 1:
        pairs = [
            pair_coefs(gram[i][i + 1], gram[i][i], gram[i + 1][i + 1])
            for i in range(0, len(gram), 2)
        ]
        for member in range(count):
            coefs[member] = coefs[member] * pairs[member // (2 * span)][member // span % 2]
        half = len(gram) // 2
        merged = [[None] * half for _ in range(half)]
        for i in range(half):
            for j in range(half):
                merged[i][j] = sum(
                    pairs[i][a] * pairs[j][b] * gram[2 * i + a][2 * j + b]
                    for a in range(2)
                    for b in range(2)
                )
        gram = merged
        span *= 2
    return coefs


def norm_bound(coefs, squares):
    bound = jnp.abs(coefs[0]) * jnp.sqrt(squares[0]) + jnp.abs(coefs[1]) * jnp.sqrt(squares[1])
    return jnp.maximum(bound, TINY_BOUND)


def move(block, route):
    return lax.ppermute(block, "rep", route)


def settle_kernel(plan, span, shard_count, *refs):
    blocks = refs[: plan.blocks]
    extras = refs[plan.blocks : plan.blocks + plan.extras]
    outs = refs[plan.blocks + plan.extras : -5]
    acc, payload, inbox, send_sem, recv_sem = refs[-5:]
    step = pl.program_id(0)
    rep = lax.axis_index("rep")
    shard = lax.axis_index("shard")
    inside = lax.rem(rep, span)
    peers = []
    for far in range(shard_count):
        for near in range(span):
            if far or near:
                target = rep - inside + lax.rem(inside + near, span)
                peers.append((far * span + near, (lax.rem(shard + far, shard_count), target)))
    barrier = pltpu.get_barrier_semaphore()

    @pl.when(step == 0)
    def _():
        acc[...] = jnp.zeros_like(acc)
        for _, peer in peers:
            pl.semaphore_signal(
                barrier, inc=1, device_id=peer, device_id_type=pl.DeviceIdType.MESH
            )

    views = [ref[...].reshape(-1, 8, ref.shape[-1]) for ref in blocks]
    for number, (left, right) in enumerate(plan.products):
        acc[number] += jnp.sum(views[left] * views[right], axis=0)

    @pl.when(step == pl.num_programs(0) - 1)
    def _():
        flat = lax.broadcasted_iota(jnp.int32, TILE, 0) * TILE[1]
        flat = flat + lax.broadcasted_iota(jnp.int32, TILE, 1)
        sums = [
            jnp.sum(jnp.sum(acc[number], axis=0, keepdims=True), axis=1, keepdims=True)
            for number in range(len(plan.products))
        ]
        tile = jnp.zeros(TILE, jnp.float32)
        for place, value in plan.place(sums, [ref[...] for ref in extras], rep, shard):
            tile = jnp.where(flat == place, value, tile)
        payload[...] = tile
        pl.semaphore_wait(barrier, len(peers))
        copies = [
            pltpu.make_async_remote_copy(
                src_ref=payload,
                dst_ref=inbox.at[slot],
                send_sem=send_sem.at[slot],
                recv_sem=recv_sem.at[slot],
                device_id=peer,
                device_id_type=pl.DeviceIdType.MESH,
            )
            for slot, peer in peers
        ]
        for copy in copies:
            copy.start()
        for copy in copies:
            copy.wait()
        total = payload[...]
        for slot, _ in peers:
            total = total + inbox[slot]

        def read(place):
            masked = jnp.where(flat == place, total, 0.0)
            return jnp.sum(jnp.sum(masked, axis=0, keepdims=True), axis=1, keepdims=True)

        for out, value in zip(outs, plan.finish(read, rep), strict=True):
            out[...] = value


class Plan:
    def __init__(self, blocks, products, extras, place, finish, outs):
        self.blocks, self.products, self.extras = blocks, products, extras
        self.place, self.finish, self.outs = place, finish, outs


def settle(plan, span, shard_count, steps, specs, operands, extras, features, identity):
    slots = span * shard_count
    unit = jax.ShapeDtypeStruct((1, 1), jnp.float32)
    whole = pl.BlockSpec((1, 1), lambda i: (0, 0))
    results = pl.pallas_call(
        functools.partial(settle_kernel, plan, span, shard_count),
        grid=(steps,),
        out_shape=[unit] * plan.outs,
        in_specs=specs + [whole] * plan.extras,
        out_specs=[whole] * plan.outs,
        scratch_shapes=[
            pltpu.VMEM((len(plan.products), 8, features), jnp.float32),
            pltpu.VMEM(TILE, jnp.float32),
            pltpu.VMEM((slots,) + TILE, jnp.float32),
            pltpu.SemaphoreType.DMA((slots,)),
            pltpu.SemaphoreType.DMA((slots,)),
        ],
        compiler_params=pltpu.CompilerParams(collective_id=identity, has_side_effects=True),
    )(*operands, *extras)
    return [result.reshape(()) for result in results]


DUEL = [(0, 1), (0, 0), (1, 1)]


def sided(is_first, own, other):
    return jnp.where(is_first, own, other), jnp.where(is_first, other, own)


def core_plan():
    def place(sums, extras, rep, shard):
        is_first = lax.rem(rep, 2) == 0
        for base in (0, 3):
            first, second = sided(is_first, sums[base + 1], sums[base + 2])
            yield from ((base, sums[base]), (base + 1, first), (base + 2, second))

    def finish(read, rep):
        is_first = lax.rem(rep, 2) == 0
        for base in (0, 3):
            squares = (read(base + 1), read(base + 2))
            first, second = pair_coefs(read(base), *squares)
            scale = norm_bound((first, second), squares) / HALF_TOP
            own, other = sided(is_first, first / scale, second / scale)
            yield from (own, other, scale)

    products = DUEL + [(a + 2, b + 2) for a, b in DUEL]
    return Plan(4, products, 0, place, finish, 6)


def owns(rep, shard, members):
    return (shard == 0) & (lax.rem(rep, members) == 0)


def duo_plan():
    def place(sums, extras, rep, shard):
        even = lax.rem(rep // 2, 2) == 0
        first, second = sided(even, sums[1], sums[2])
        yield from ((0, sums[0]), (1, first), (2, second))
        mine = jnp.where(owns(rep, shard, 2), extras[0], 0.0)
        low, high = sided(even, mine, jnp.zeros_like(mine))
        yield from ((3, low), (4, high))

    def finish(read, rep):
        even = lax.rem(rep // 2, 2) == 0
        low, high = read(3), read(4)
        squares = (read(1) * (low * low), read(2) * (high * high))
        first, second = pair_coefs(read(0) * (low * high), *squares)
        scale = norm_bound((first, second), squares) / HALF_TOP
        own, other = sided(even, first * low / scale, second * high / scale)
        yield from (own, other, scale)

    return Plan(2, DUEL, 1, place, finish, 3)


def final_plan(counts, members):
    bases = (0, counts[0] * (counts[0] + 1))
    offsets = (0, counts[0])
    products = [
        (offset + i, offset + j)
        for offset, count in zip(offsets, counts)
        for i in range(count)
        for j in range(i, count)
    ]

    def place(sums, extras, rep, shard):
        number = 0
        for base, count, size, scale in zip(bases, counts, members, extras):
            unit = rep // size
            for i in range(count):
                for j in range(i, count):
                    left = lax.rem(unit - i + count, count)
                    right = lax.rem(unit - j + count, count)
                    low, high = jnp.minimum(left, right), jnp.maximum(left, right)
                    yield base + low * count + high, sums[number]
                    number += 1
            mine = jnp.where(owns(rep, shard, size), scale, 0.0)
            yield base + count * count + unit, mine

    def finish(read, rep):
        for base, count, size in zip(bases, counts, members):
            unit = rep // size
            scales = [read(base + count * count + i) for i in range(count)]
            gram = [[None] * count for _ in range(count)]
            for i in range(count):
                for j in range(i, count):
                    gram[i][j] = read(base + i * count + j) * (scales[i] * scales[j])
                    gram[j][i] = gram[i][j]
            coefs = tree_coefs(gram)
            weights = [coef * scale for coef, scale in zip(coefs, scales)]
            for step in range(count):
                source = lax.rem(unit - step + count, count)
                chosen = weights[0]
                for i in range(1, count):
                    chosen = jnp.where(source == i, weights[i], chosen)
                yield chosen

    return Plan(sum(counts), products, len(counts), place, finish, sum(counts))


def shards(
    tokens, key_cotangent, value_cotangent, key_weight, value_weight, key_moment, value_moment
):
    replicas = lax.axis_size("rep")
    shard_count = lax.axis_size("shard")
    device_index = lax.axis_index("rep")
    groups = replicas // 2
    duos = groups // 2
    core = device_index % 2
    group = device_index // 2
    half_bit = group % 2
    duo = group // 2
    width, features = tokens.shape[1], key_cotangent.shape[1]
    block = width // replicas
    factor = 1.0 / math.sqrt(tokens.shape[0])

    def grad(cotangent):
        product = lax.dot_general(
            tokens, cotangent, (((0,), (0,)), ((), ())), preferred_element_type=jnp.float32
        )
        return (product * factor).reshape(groups, 2, block, features)

    def swap_cores(full):
        outgoing = lax.dynamic_index_in_dim(full, 1 - core, 1, keepdims=False)
        return move(outgoing, [(i, i ^ 1) for i in range(replicas)])

    value_full = grad(value_cotangent)
    value_arrived = swap_cores(value_full)
    key_full = grad(key_cotangent)
    key_arrived = swap_cores(key_full)

    mine = pl.BlockSpec(
        (None, None, block, features), lambda i: (i, lax.rem(lax.axis_index("rep"), 2), 0, 0)
    )
    theirs = pl.BlockSpec((None, block, features), lambda i: (i, 0, 0))
    value_own, value_other, value_scale, key_own, key_other, key_scale = settle(
        core_plan(), 2, shard_count, groups, [mine, theirs] * 2,
        [value_full, value_arrived, key_full, key_arrived], [], features, 0,
    )

    def merged_block(full, arrived, own, other, target):
        kept = lax.dynamic_slice(full, (target, core, 0, 0), (1, 1, block, features))
        came = lax.dynamic_slice(arrived, (target, 0, 0), (1, block, features))
        return own * kept.reshape(block, features) + other * came.reshape(block, features)

    def half_blocks(bit):
        kept = value_full.reshape(duos, 2, 2, block, features)
        kept = lax.dynamic_slice(kept, (0, bit, core, 0, 0), (duos, 1, 1, block, features))
        came = value_arrived.reshape(duos, 2, block, features)
        came = lax.dynamic_slice(came, (0, bit, 0, 0), (duos, 1, block, features))
        shape = (duos, block, features)
        return value_own * kept.reshape(shape) + value_other * came.reshape(shape)

    outgoing = lax.optimization_barrier(half_blocks(1 - half_bit).astype(HALF))
    arrived = move(outgoing, [(i, i ^ 2) for i in range(replicas)])

    key_blocks = [merged_block(key_full, key_arrived, key_own, key_other, group)]
    for step in range(1, groups):
        route = [
            (2 * g + c, 2 * ((g + step) % groups) + c) for g in range(groups) for c in range(2)
        ]
        target = lax.rem(group + step, groups)
        sent = merged_block(key_full, key_arrived, key_own, key_other, target).astype(HALF)
        key_blocks.append(move(lax.optimization_barrier(sent), route).astype(jnp.float32))

    kept = half_blocks(half_bit)
    arrived = arrived.astype(jnp.float32)
    units = pl.BlockSpec((None, block, features), lambda i: (i, 0, 0))
    duo_own, duo_other, duo_scale = settle(
        duo_plan(), 4, shard_count, duos, [units] * 2, [kept, arrived],
        [value_scale.reshape(1, 1)], features, 1,
    )

    def duo_block(target):
        ours = lax.dynamic_index_in_dim(kept, target, 0, keepdims=False)
        came = lax.dynamic_index_in_dim(arrived, target, 0, keepdims=False)
        return duo_own * ours + duo_other * came

    value_blocks = [duo_block(duo)]
    for step in range(1, duos):
        route = [
            (4 * d + c, 4 * ((d + step) % duos) + c) for d in range(duos) for c in range(4)
        ]
        sent = duo_block(lax.rem(duo + step, duos)).astype(HALF)
        value_blocks.append(move(lax.optimization_barrier(sent), route).astype(jnp.float32))

    rows = pl.BlockSpec((block // 2, features), lambda i: (i, 0))
    weights = settle(
        final_plan((groups, duos), (2, 4)), replicas, shard_count, 2, [rows] * (groups + duos),
        key_blocks + value_blocks, [key_scale.reshape(1, 1), duo_scale.reshape(1, 1)], features, 2,
    )
    key_merged = sum(w * b for w, b in zip(weights[:groups], key_blocks))
    value_merged = sum(w * b for w, b in zip(weights[groups:], value_blocks))

    new_key_moment = MOMENTUM_DECAY * key_moment + key_merged
    new_value_moment = MOMENTUM_DECAY * value_moment + value_merged
    new_key_weight = key_weight - STEP_SIZE * new_key_moment
    new_value_weight = value_weight - STEP_SIZE * new_value_moment
    return (new_key_weight, new_value_weight, new_key_moment, new_value_moment)


def solution(mesh):
    grads = (P("rep", None),) * 2
    rows = (P(("shard", "rep"), None),) * 4
    return jax.shard_map(
        shards, mesh=mesh, in_specs=(P("rep", "shard"),) + grads + rows, out_specs=rows,
        check_vma=False,
    )
```

```python
import functools
import math

import jax
import jax.numpy as jnp
from jax import lax
from jax.experimental import pallas as pl
from jax.experimental.pallas import tpu as pltpu
from jax.sharding import PartitionSpec as P

EPSILON = 1e-06
MOMENTUM_DECAY = 0.9
STEP_SIZE = 0.01
TINY_BOUND = 1e-16
HALF_TOP = 32768.0
HALF = jnp.float16
TILE = (8, 128)


def pair_coefs(cross, first_square, second_square):
    first = 1.0 - cross / (2.0 * (first_square + EPSILON))
    second = 1.0 - cross / (2.0 * (second_square + EPSILON))
    return first, second


def tree_coefs(gram):
    count = len(gram)
    coefs = [1.0] * count
    span = 1
    while len(gram) > 1:
        pairs = [
            pair_coefs(gram[i][i + 1], gram[i][i], gram[i + 1][i + 1])
            for i in range(0, len(gram), 2)
        ]
        for member in range(count):
            coefs[member] = coefs[member] * pairs[member // (2 * span)][member // span % 2]
        half = len(gram) // 2
        merged = [[None] * half for _ in range(half)]
        for i in range(half):
            for j in range(half):
                merged[i][j] = sum(
                    pairs[i][a] * pairs[j][b] * gram[2 * i + a][2 * j + b]
                    for a in range(2)
                    for b in range(2)
                )
        gram = merged
        span *= 2
    return coefs


def norm_bound(coefs, squares):
    bound = jnp.abs(coefs[0]) * jnp.sqrt(squares[0]) + jnp.abs(coefs[1]) * jnp.sqrt(squares[1])
    return jnp.maximum(bound, TINY_BOUND)


def move(block, route):
    return lax.ppermute(block, "rep", route)


def settle_kernel(plan, span, shard_count, *refs):
    blocks = refs[: plan.blocks]
    extras = refs[plan.blocks : plan.blocks + plan.extras]
    outs = refs[plan.blocks + plan.extras + plan.waits : -5]
    acc, payload, inbox, send_sem, recv_sem = refs[-5:]
    step = pl.program_id(0)
    rep = lax.axis_index("rep")
    shard = lax.axis_index("shard")
    inside = lax.rem(rep, span)
    peers = []
    for far in range(shard_count):
        for near in range(span):
            if far or near:
                target = rep - inside + lax.rem(inside + near, span)
                peers.append((far * span + near, (lax.rem(shard + far, shard_count), target)))
    barrier = pltpu.get_barrier_semaphore()

    @pl.when(step == 0)
    def _():
        acc[...] = jnp.zeros_like(acc)
        for _, peer in peers:
            pl.semaphore_signal(
                barrier, inc=1, device_id=peer, device_id_type=pl.DeviceIdType.MESH
            )

    views = [ref[...].reshape(-1, 8, ref.shape[-1]) for ref in blocks]
    for number, (left, right) in enumerate(plan.products):
        acc[number] += jnp.sum(views[left] * views[right], axis=0)

    @pl.when(step == pl.num_programs(0) - 1)
    def _():
        flat = lax.broadcasted_iota(jnp.int32, TILE, 0) * TILE[1]
        flat = flat + lax.broadcasted_iota(jnp.int32, TILE, 1)
        sums = [
            jnp.sum(jnp.sum(acc[number], axis=0, keepdims=True), axis=1, keepdims=True)
            for number in range(len(plan.products))
        ]
        tile = jnp.zeros(TILE, jnp.float32)
        for place, value in plan.place(sums, [ref[...] for ref in extras], rep, shard):
            tile = jnp.where(flat == place, value, tile)
        payload[...] = tile
        pl.semaphore_wait(barrier, len(peers))
        copies = [
            pltpu.make_async_remote_copy(
                src_ref=payload,
                dst_ref=inbox.at[slot],
                send_sem=send_sem.at[slot],
                recv_sem=recv_sem.at[slot],
                device_id=peer,
                device_id_type=pl.DeviceIdType.MESH,
            )
            for slot, peer in peers
        ]
        for copy in copies:
            copy.start()
        for copy in copies:
            copy.wait()
        total = payload[...]
        for slot, _ in peers:
            total = total + inbox[slot]

        def read(place):
            masked = jnp.where(flat == place, total, 0.0)
            return jnp.sum(jnp.sum(masked, axis=0, keepdims=True), axis=1, keepdims=True)

        for out, value in zip(outs, plan.finish(read, rep), strict=True):
            out[...] = value


class Plan:
    def __init__(self, blocks, products, extras, place, finish, outs):
        self.blocks, self.products, self.extras, self.waits = blocks, products, extras, 0
        self.place, self.finish, self.outs = place, finish, outs


def settle(plan, span, shard_count, steps, specs, operands, extras, features, identity, after=()):
    plan.waits = len(after)
    slots = span * shard_count
    unit = jax.ShapeDtypeStruct((1, 1), jnp.float32)
    whole = pl.BlockSpec((1, 1), lambda i: (0, 0))
    results = pl.pallas_call(
        functools.partial(settle_kernel, plan, span, shard_count),
        grid=(steps,),
        out_shape=[unit] * plan.outs,
        in_specs=specs + [whole] * plan.extras + [pl.BlockSpec(memory_space=pl.ANY)] * plan.waits,
        out_specs=[whole] * plan.outs,
        scratch_shapes=[
            pltpu.VMEM((len(plan.products), 8, features), jnp.float32),
            pltpu.VMEM(TILE, jnp.float32),
            pltpu.VMEM((slots,) + TILE, jnp.float32),
            pltpu.SemaphoreType.DMA((slots,)),
            pltpu.SemaphoreType.DMA((slots,)),
        ],
        compiler_params=pltpu.CompilerParams(collective_id=identity, has_side_effects=True),
    )(*operands, *extras, *after)
    return [result.reshape(()) for result in results]


DUEL = [(0, 1), (0, 0), (1, 1)]


def sided(is_first, own, other):
    return jnp.where(is_first, own, other), jnp.where(is_first, other, own)


def core_plan():
    def place(sums, extras, rep, shard):
        first, second = sided(lax.rem(rep, 2) == 0, sums[1], sums[2])
        yield from ((0, sums[0]), (1, first), (2, second))

    def finish(read, rep):
        squares = (read(1), read(2))
        first, second = pair_coefs(read(0), *squares)
        scale = norm_bound((first, second), squares) / HALF_TOP
        own, other = sided(lax.rem(rep, 2) == 0, first / scale, second / scale)
        yield from (own, other, scale)

    return Plan(2, DUEL, 0, place, finish, 3)


def owns(rep, shard, members):
    return (shard == 0) & (lax.rem(rep, members) == 0)


def duo_plan():
    def place(sums, extras, rep, shard):
        even = lax.rem(rep // 2, 2) == 0
        first, second = sided(even, sums[1], sums[2])
        yield from ((0, sums[0]), (1, first), (2, second))
        mine = jnp.where(owns(rep, shard, 2), extras[0], 0.0)
        low, high = sided(even, mine, jnp.zeros_like(mine))
        yield from ((3, low), (4, high))

    def finish(read, rep):
        even = lax.rem(rep // 2, 2) == 0
        low, high = read(3), read(4)
        squares = (read(1) * (low * low), read(2) * (high * high))
        first, second = pair_coefs(read(0) * (low * high), *squares)
        scale = norm_bound((first, second), squares) / HALF_TOP
        own, other = sided(even, first * low / scale, second * high / scale)
        yield from (own, other, scale, jnp.ones_like(scale))

    return Plan(2, DUEL, 1, place, finish, 4)


def final_plan(count, size):
    products = [(i, j) for i in range(count) for j in range(i, count)]

    def place(sums, extras, rep, shard):
        unit = rep // size
        for (i, j), value in zip(products, sums):
            left = lax.rem(unit - i + count, count)
            right = lax.rem(unit - j + count, count)
            low, high = jnp.minimum(left, right), jnp.maximum(left, right)
            yield low * count + high, value
        yield count * count + unit, jnp.where(owns(rep, shard, size), extras[0], 0.0)

    def finish(read, rep):
        unit = rep // size
        scales = [read(count * count + i) for i in range(count)]
        gram = [[None] * count for _ in range(count)]
        for i, j in products:
            gram[i][j] = read(i * count + j) * (scales[i] * scales[j])
            gram[j][i] = gram[i][j]
        weights = [coef * scale for coef, scale in zip(tree_coefs(gram), scales)]
        for step in range(count):
            source = lax.rem(unit - step + count, count)
            chosen = weights[0]
            for i in range(1, count):
                chosen = jnp.where(source == i, weights[i], chosen)
            yield chosen

    return Plan(count, products, 1, place, finish, count)


def shards(
    tokens, key_cotangent, value_cotangent, key_weight, value_weight, key_moment, value_moment
):
    replicas = lax.axis_size("rep")
    shard_count = lax.axis_size("shard")
    device_index = lax.axis_index("rep")
    groups = replicas // 2
    duos = groups // 2
    core = device_index % 2
    group = device_index // 2
    half_bit = group % 2
    duo = group // 2
    width, features = tokens.shape[1], key_cotangent.shape[1]
    block = width // replicas
    factor = 1.0 / math.sqrt(tokens.shape[0])

    def grad(cotangent):
        product = lax.dot_general(
            tokens, cotangent, (((0,), (0,)), ((), ())), preferred_element_type=jnp.float32
        )
        return (product * factor).reshape(groups, 2, block, features)

    def swap_cores(full):
        outgoing = lax.dynamic_index_in_dim(full, 1 - core, 1, keepdims=False)
        return move(outgoing, [(i, i ^ 1) for i in range(replicas)])

    value_full = grad(value_cotangent)
    value_arrived = swap_cores(value_full)
    key_full = grad(key_cotangent)
    key_arrived = swap_cores(key_full)

    mine = pl.BlockSpec(
        (None, None, block, features), lambda i: (i, lax.rem(lax.axis_index("rep"), 2), 0, 0)
    )
    theirs = pl.BlockSpec((None, block, features), lambda i: (i, 0, 0))
    value_own, value_other, value_scale = settle(
        core_plan(), 2, shard_count, groups, [mine, theirs], [value_full, value_arrived], [],
        features, 0,
    )

    def merged_block(full, arrived, own, other, target):
        kept = lax.dynamic_slice(full, (target, core, 0, 0), (1, 1, block, features))
        came = lax.dynamic_slice(arrived, (target, 0, 0), (1, block, features))
        return own * kept.reshape(block, features) + other * came.reshape(block, features)

    def half_blocks(bit, own, other):
        kept = value_full.reshape(duos, 2, 2, block, features)
        kept = lax.dynamic_slice(kept, (0, bit, core, 0, 0), (duos, 1, 1, block, features))
        came = value_arrived.reshape(duos, 2, block, features)
        came = lax.dynamic_slice(came, (0, bit, 0, 0), (duos, 1, block, features))
        shape = (duos, block, features)
        return own * kept.reshape(shape) + other * came.reshape(shape)

    outgoing = half_blocks(1 - half_bit, value_own, value_other).astype(HALF)
    outgoing, value_own, value_other = lax.optimization_barrier(
        (outgoing, value_own, value_other)
    )
    arrived = move(outgoing, [(i, i ^ 2) for i in range(replicas)])

    key_own, key_other, key_scale = settle(
        core_plan(), 2, shard_count, groups, [mine, theirs], [key_full, key_arrived], [],
        features, 1, [value_own.reshape(1, 1)],
    )
    came = {}
    for step in sorted(range(1, groups), key=lambda s: -min(s, groups - s)):
        route = [
            (2 * g + c, 2 * ((g + step) % groups) + c) for g in range(groups) for c in range(2)
        ]
        target = lax.rem(group + step, groups)
        sent = merged_block(key_full, key_arrived, key_own, key_other, target).astype(HALF)
        sent, key_own, key_other = lax.optimization_barrier((sent, key_own, key_other))
        came[step] = move(sent, route)
    key_block = merged_block(key_full, key_arrived, key_own, key_other, group)
    key_came = came

    kept = half_blocks(half_bit, value_own, value_other)
    arrived = arrived.astype(jnp.float32)
    units = pl.BlockSpec((None, block, features), lambda i: (i, 0, 0))
    duo_own, duo_other, duo_scale, one = settle(
        duo_plan(), 4, shard_count, duos, [units] * 2, [kept, arrived],
        [value_scale.reshape(1, 1)], features, 2,
    )

    def duo_block(target, duo_own, duo_other):
        ours = lax.dynamic_index_in_dim(kept, target, 0, keepdims=False)
        came = lax.dynamic_index_in_dim(arrived, target, 0, keepdims=False)
        return duo_own * ours + duo_other * came

    came = []
    for step in range(1, duos):
        route = [
            (4 * d + c, 4 * ((d + step) % duos) + c) for d in range(duos) for c in range(4)
        ]
        sent = duo_block(lax.rem(duo + step, duos), duo_own, duo_other).astype(HALF)
        sent, duo_own, duo_other, one = lax.optimization_barrier((sent, duo_own, duo_other, one))
        came.append(move(sent, route))
    key_blocks = [key_block]
    key_blocks += [key_came[step].astype(jnp.float32) * one for step in range(1, groups)]
    value_blocks = [duo_block(duo, duo_own, duo_other)]
    value_blocks += [block_came.astype(jnp.float32) for block_came in came]

    rows = pl.BlockSpec((block // 2, features), lambda i: (i, 0))

    def finish(count, size, blocks, scale, identity, after, moment, weight):
        weights = settle(
            final_plan(count, size), replicas, shard_count, 2, [rows] * count, blocks,
            [scale.reshape(1, 1)], features, identity, after,
        )
        new_moment = MOMENTUM_DECAY * moment + sum(w * b for w, b in zip(weights, blocks))
        return new_moment, weight - STEP_SIZE * new_moment

    new_key_moment, new_key_weight = finish(
        groups, 2, key_blocks, key_scale, 3, [duo_own.reshape(1, 1)], key_moment, key_weight
    )
    new_value_moment, new_value_weight = finish(
        duos, 4, value_blocks, duo_scale, 4, [], value_moment, value_weight
    )
    return (new_key_weight, new_value_weight, new_key_moment, new_value_moment)


def solution(mesh):
    grads = (P("rep", None),) * 2
    rows = (P(("shard", "rep"), None),) * 4
    return jax.shard_map(
        shards, mesh=mesh, in_specs=(P("rep", "shard"),) + grads + rows, out_specs=rows,
        check_vma=False,
    )
```

```python
import functools
import math

import jax
import jax.numpy as jnp
from jax import lax
from jax.experimental import pallas as pl
from jax.experimental.pallas import tpu as pltpu
from jax.sharding import PartitionSpec as P

EPSILON = 1e-06
MOMENTUM_DECAY = 0.9
STEP_SIZE = 0.01
TINY_BOUND = 1e-16
HALF_TOP = 32768.0
HALF = jnp.float16
TILE = (8, 128)


def pair_coefs(cross, first_square, second_square):
    first = 1.0 - cross / (2.0 * (first_square + EPSILON))
    second = 1.0 - cross / (2.0 * (second_square + EPSILON))
    return first, second


def tree_coefs(gram):
    count = len(gram)
    coefs = [1.0] * count
    span = 1
    while len(gram) > 1:
        pairs = [
            pair_coefs(gram[i][i + 1], gram[i][i], gram[i + 1][i + 1])
            for i in range(0, len(gram), 2)
        ]
        for member in range(count):
            coefs[member] = coefs[member] * pairs[member // (2 * span)][member // span % 2]
        half = len(gram) // 2
        merged = [[None] * half for _ in range(half)]
        for i in range(half):
            for j in range(half):
                merged[i][j] = sum(
                    pairs[i][a] * pairs[j][b] * gram[2 * i + a][2 * j + b]
                    for a in range(2)
                    for b in range(2)
                )
        gram = merged
        span *= 2
    return coefs


def norm_bound(coefs, squares):
    bound = jnp.abs(coefs[0]) * jnp.sqrt(squares[0]) + jnp.abs(coefs[1]) * jnp.sqrt(squares[1])
    return jnp.maximum(bound, TINY_BOUND)


def move(block, route):
    return lax.ppermute(block, "rep", route)


def settle_kernel(plan, span, shard_count, *refs):
    blocks = refs[: plan.blocks]
    extras = refs[plan.blocks : plan.blocks + plan.extras]
    outs = refs[plan.blocks + plan.extras + plan.waits : -5]
    acc, payload, inbox, send_sem, recv_sem = refs[-5:]
    step = pl.program_id(0)
    rep = lax.axis_index("rep")
    shard = lax.axis_index("shard")
    inside = lax.rem(rep, span)
    peers = []
    for far in range(shard_count):
        for near in range(span):
            if far or near:
                target = rep - inside + lax.rem(inside + near, span)
                peers.append((far * span + near, (lax.rem(shard + far, shard_count), target)))
    barrier = pltpu.get_barrier_semaphore()

    @pl.when(step == 0)
    def _():
        acc[...] = jnp.zeros_like(acc)
        for _, peer in peers:
            pl.semaphore_signal(
                barrier, inc=1, device_id=peer, device_id_type=pl.DeviceIdType.MESH
            )

    views = [ref[...].reshape(-1, 8, ref.shape[-1]) for ref in blocks]
    for number, (left, right) in enumerate(plan.products):
        acc[number] += jnp.sum(views[left] * views[right], axis=0)

    @pl.when(step == pl.num_programs(0) - 1)
    def _():
        flat = lax.broadcasted_iota(jnp.int32, TILE, 0) * TILE[1]
        flat = flat + lax.broadcasted_iota(jnp.int32, TILE, 1)
        sums = [
            jnp.sum(jnp.sum(acc[number], axis=0, keepdims=True), axis=1, keepdims=True)
            for number in range(len(plan.products))
        ]
        tile = jnp.zeros(TILE, jnp.float32)
        for place, value in plan.place(sums, [ref[...] for ref in extras], rep, shard):
            tile = jnp.where(flat == place, value, tile)
        payload[...] = tile
        pl.semaphore_wait(barrier, len(peers))
        copies = [
            pltpu.make_async_remote_copy(
                src_ref=payload,
                dst_ref=inbox.at[slot],
                send_sem=send_sem.at[slot],
                recv_sem=recv_sem.at[slot],
                device_id=peer,
                device_id_type=pl.DeviceIdType.MESH,
            )
            for slot, peer in peers
        ]
        for copy in copies:
            copy.start()
        for copy in copies:
            copy.wait()
        total = payload[...]
        for slot, _ in peers:
            total = total + inbox[slot]

        def read(place):
            masked = jnp.where(flat == place, total, 0.0)
            return jnp.sum(jnp.sum(masked, axis=0, keepdims=True), axis=1, keepdims=True)

        for out, value in zip(outs, plan.finish(read, rep), strict=True):
            out[...] = value


class Plan:
    def __init__(self, blocks, products, extras, place, finish, outs):
        self.blocks, self.products, self.extras, self.waits = blocks, products, extras, 0
        self.place, self.finish, self.outs = place, finish, outs


def settle(plan, span, shard_count, steps, specs, operands, extras, features, identity, after=()):
    plan.waits = len(after)
    slots = span * shard_count
    unit = jax.ShapeDtypeStruct((1, 1), jnp.float32)
    whole = pl.BlockSpec((1, 1), lambda i: (0, 0))
    results = pl.pallas_call(
        functools.partial(settle_kernel, plan, span, shard_count),
        grid=(steps,),
        out_shape=[unit] * plan.outs,
        in_specs=specs + [whole] * plan.extras + [pl.BlockSpec(memory_space=pl.ANY)] * plan.waits,
        out_specs=[whole] * plan.outs,
        scratch_shapes=[
            pltpu.VMEM((len(plan.products), 8, features), jnp.float32),
            pltpu.VMEM(TILE, jnp.float32),
            pltpu.VMEM((slots,) + TILE, jnp.float32),
            pltpu.SemaphoreType.DMA((slots,)),
            pltpu.SemaphoreType.DMA((slots,)),
        ],
        compiler_params=pltpu.CompilerParams(collective_id=identity, has_side_effects=True),
    )(*operands, *extras, *after)
    return [result.reshape(()) for result in results]


DUEL = [(0, 1), (0, 0), (1, 1)]


def sided(is_first, own, other):
    return jnp.where(is_first, own, other), jnp.where(is_first, other, own)


def core_plan():
    def place(sums, extras, rep, shard):
        first, second = sided(lax.rem(rep, 2) == 0, sums[1], sums[2])
        yield from ((0, sums[0]), (1, first), (2, second))

    def finish(read, rep):
        squares = (read(1), read(2))
        first, second = pair_coefs(read(0), *squares)
        scale = norm_bound((first, second), squares) / HALF_TOP
        own, other = sided(lax.rem(rep, 2) == 0, first / scale, second / scale)
        yield from (own, other, scale)

    return Plan(2, DUEL, 0, place, finish, 3)


def owns(rep, shard, members):
    return (shard == 0) & (lax.rem(rep, members) == 0)


def duo_plan():
    def place(sums, extras, rep, shard):
        even = lax.rem(rep // 2, 2) == 0
        first, second = sided(even, sums[1], sums[2])
        yield from ((0, sums[0]), (1, first), (2, second))
        mine = jnp.where(owns(rep, shard, 2), extras[0], 0.0)
        low, high = sided(even, mine, jnp.zeros_like(mine))
        yield from ((3, low), (4, high))

    def finish(read, rep):
        even = lax.rem(rep // 2, 2) == 0
        low, high = read(3), read(4)
        squares = (read(1) * (low * low), read(2) * (high * high))
        first, second = pair_coefs(read(0) * (low * high), *squares)
        scale = norm_bound((first, second), squares) / HALF_TOP
        own, other = sided(even, first * low / scale, second * high / scale)
        yield from (own, other, scale, jnp.ones_like(scale))

    return Plan(2, DUEL, 1, place, finish, 4)


def final_plan(counts, members):
    bases = (0, counts[0] * (counts[0] + 1))
    offsets = (0, counts[0])
    products = [
        (offset + i, offset + j)
        for offset, count in zip(offsets, counts)
        for i in range(count)
        for j in range(i, count)
    ]

    def place(sums, extras, rep, shard):
        number = 0
        for base, count, size, scale in zip(bases, counts, members, extras):
            unit = rep // size
            for i in range(count):
                for j in range(i, count):
                    left = lax.rem(unit - i + count, count)
                    right = lax.rem(unit - j + count, count)
                    low, high = jnp.minimum(left, right), jnp.maximum(left, right)
                    yield base + low * count + high, sums[number]
                    number += 1
            mine = jnp.where(owns(rep, shard, size), scale, 0.0)
            yield base + count * count + unit, mine

    def finish(read, rep):
        for base, count, size in zip(bases, counts, members):
            unit = rep // size
            scales = [read(base + count * count + i) for i in range(count)]
            gram = [[None] * count for _ in range(count)]
            for i in range(count):
                for j in range(i, count):
                    gram[i][j] = read(base + i * count + j) * (scales[i] * scales[j])
                    gram[j][i] = gram[i][j]
            coefs = tree_coefs(gram)
            weights = [coef * scale for coef, scale in zip(coefs, scales)]
            for step in range(count):
                source = lax.rem(unit - step + count, count)
                chosen = weights[0]
                for i in range(1, count):
                    chosen = jnp.where(source == i, weights[i], chosen)
                yield chosen

    return Plan(sum(counts), products, len(counts), place, finish, sum(counts))


def shards(
    tokens, key_cotangent, value_cotangent, key_weight, value_weight, key_moment, value_moment
):
    replicas = lax.axis_size("rep")
    shard_count = lax.axis_size("shard")
    device_index = lax.axis_index("rep")
    groups = replicas // 2
    duos = groups // 2
    core = device_index % 2
    group = device_index // 2
    half_bit = group % 2
    duo = group // 2
    width, features = tokens.shape[1], key_cotangent.shape[1]
    block = width // replicas
    factor = 1.0 / math.sqrt(tokens.shape[0])

    def grad(cotangent):
        product = lax.dot_general(
            tokens, cotangent, (((0,), (0,)), ((), ())), preferred_element_type=jnp.float32
        )
        return (product * factor).reshape(groups, 2, block, features)

    def swap_cores(full):
        outgoing = lax.dynamic_index_in_dim(full, 1 - core, 1, keepdims=False)
        return move(outgoing, [(i, i ^ 1) for i in range(replicas)])

    value_full = grad(value_cotangent)
    value_arrived = swap_cores(value_full)
    key_full = grad(key_cotangent)
    key_arrived = swap_cores(key_full)

    mine = pl.BlockSpec(
        (None, None, block, features), lambda i: (i, lax.rem(lax.axis_index("rep"), 2), 0, 0)
    )
    theirs = pl.BlockSpec((None, block, features), lambda i: (i, 0, 0))
    value_own, value_other, value_scale = settle(
        core_plan(), 2, shard_count, groups, [mine, theirs], [value_full, value_arrived], [],
        features, 0,
    )

    def merged_block(full, arrived, own, other, target):
        kept = lax.dynamic_slice(full, (target, core, 0, 0), (1, 1, block, features))
        came = lax.dynamic_slice(arrived, (target, 0, 0), (1, block, features))
        return own * kept.reshape(block, features) + other * came.reshape(block, features)

    def half_blocks(bit, own, other):
        kept = value_full.reshape(duos, 2, 2, block, features)
        kept = lax.dynamic_slice(kept, (0, bit, core, 0, 0), (duos, 1, 1, block, features))
        came = value_arrived.reshape(duos, 2, block, features)
        came = lax.dynamic_slice(came, (0, bit, 0, 0), (duos, 1, block, features))
        shape = (duos, block, features)
        return own * kept.reshape(shape) + other * came.reshape(shape)

    outgoing = half_blocks(1 - half_bit, value_own, value_other).astype(HALF)
    outgoing, value_own, value_other = lax.optimization_barrier(
        (outgoing, value_own, value_other)
    )
    arrived = move(outgoing, [(i, i ^ 2) for i in range(replicas)])

    key_own, key_other, key_scale = settle(
        core_plan(), 2, shard_count, groups, [mine, theirs], [key_full, key_arrived], [],
        features, 1, [value_own.reshape(1, 1)],
    )
    came = {}
    for step in sorted(range(1, groups), key=lambda s: -min(s, groups - s)):
        route = [
            (2 * g + c, 2 * ((g + step) % groups) + c) for g in range(groups) for c in range(2)
        ]
        target = lax.rem(group + step, groups)
        sent = merged_block(key_full, key_arrived, key_own, key_other, target).astype(HALF)
        came[step] = move(lax.optimization_barrier(sent), route)
    key_block = merged_block(key_full, key_arrived, key_own, key_other, group)
    key_came = came

    kept = half_blocks(half_bit, value_own, value_other)
    arrived = arrived.astype(jnp.float32)
    units = pl.BlockSpec((None, block, features), lambda i: (i, 0, 0))
    duo_own, duo_other, duo_scale, one = settle(
        duo_plan(), 4, shard_count, duos, [units] * 2, [kept, arrived],
        [value_scale.reshape(1, 1)], features, 2,
    )

    def duo_block(target, duo_own, duo_other):
        ours = lax.dynamic_index_in_dim(kept, target, 0, keepdims=False)
        came = lax.dynamic_index_in_dim(arrived, target, 0, keepdims=False)
        return duo_own * ours + duo_other * came

    came = []
    for step in range(1, duos):
        route = [
            (4 * d + c, 4 * ((d + step) % duos) + c) for d in range(duos) for c in range(4)
        ]
        sent = duo_block(lax.rem(duo + step, duos), duo_own, duo_other).astype(HALF)
        sent, duo_own, duo_other, one = lax.optimization_barrier((sent, duo_own, duo_other, one))
        came.append(move(sent, route))
    key_blocks = [key_block]
    key_blocks += [key_came[step].astype(jnp.float32) * one for step in range(1, groups)]
    value_blocks = [duo_block(duo, duo_own, duo_other)]
    value_blocks += [block_came.astype(jnp.float32) for block_came in came]

    rows = pl.BlockSpec((block // 2, features), lambda i: (i, 0))

    weights = settle(
        final_plan((groups, duos), (2, 4)), replicas, shard_count, 2, [rows] * (groups + duos),
        key_blocks + value_blocks, [key_scale.reshape(1, 1), duo_scale.reshape(1, 1)], features, 3,
    )
    key_merged = sum(w * b for w, b in zip(weights[:groups], key_blocks))
    value_merged = sum(w * b for w, b in zip(weights[groups:], value_blocks))
    new_key_moment = MOMENTUM_DECAY * key_moment + key_merged
    new_value_moment = MOMENTUM_DECAY * value_moment + value_merged
    new_key_weight = key_weight - STEP_SIZE * new_key_moment
    new_value_weight = value_weight - STEP_SIZE * new_value_moment
    return (new_key_weight, new_value_weight, new_key_moment, new_value_moment)


def solution(mesh):
    grads = (P("rep", None),) * 2
    rows = (P(("shard", "rep"), None),) * 4
    return jax.shard_map(
        shards, mesh=mesh, in_specs=(P("rep", "shard"),) + grads + rows, out_specs=rows,
        check_vma=False,
    )
```
